32 devices in a mesh: req: 4 (over z), mlp: 8 (over y, x, core).
Axes of the slice: x: 2, y: 2, z: 4, core: 2. Of those that a mesh axis runs over, the one named last changes fastest.
Arguments:
- tokens: bfloat16 [1024, 5120], P(('req', 'mlp')), may hold values from -6 to 6
- modulation: float32 [16, 6, 5120], P('req'), may hold values from -3 to 3
- lengths: int32 [4, 4], P('req'), may hold values from 1 to 160, 256 in all within a row
- request_adapter: int32 [16], P('req'), may hold values from 0 to 31
- adapter_storage: int32 [32], replicated, may hold values from 0 to 31, each once
- adapter_down_weight: bfloat16 [32, 5120, 32], P('mlp'), may hold values from -0.078125 to 0.078125
- adapter_up_maps: bfloat16 [32, 2, 16, 4096], P('mlp'), may hold values from -1.5 to 1.5
- input_projection: bfloat16 [4, 5120, 4096], P(None, None, 'mlp'), may hold values from -0.078125 to 0.078125
- query_key_gains: float32 [3, 4096], P(None, 'mlp'), may hold values from 0.1 to 1.9
- positions: int32 [3, 1024], P(None, 'req'), may hold values from 0 to 63
- block_page_lookup: int32 [4, 16], P('req'), may hold values from 0 to 15, each once within a row
- output_projection: bfloat16 [2, 4096, 5120], P(None, 'mlp'), may hold values from -0.09375 to 0.09375
- cross_norm_gain: float32 [5120], replicated, may hold values from 0.1 to 1.9
- text_token_cache: bfloat16 [2, 16, 512, 4096], P(None, 'req', None, 'mlp'), may hold values from -3 to 3
- feedforward_up: bfloat16 [5120, 8192], P('req', 'mlp'), may hold values from -0.078125 to 0.078125
- feedforward_down: bfloat16 [8192, 5120], P('mlp', 'req'), may hold values from -0.0625 to 0.0625
Outputs:
- layer_out: bfloat16 [1024, 5120], P(('req', 'mlp'))
- kv_pages: bfloat16 [2, 64, 16, 4096], P(None, 'req', None, 'mlp')
The draws below stay inside these ranges and needn't reach their ends.
Inputs may be any that keep to these rules, and one draw needn't show every extreme that they name: `lengths`: row g lists the token counts of the 4 requests of group g in order; they fill the group's 256 positions, and the largest is 160. A permutation: adapter a is stored at index adapter_storage[a] of adapter_down_weight and adapter_up_maps. `block_page_lookup`: each row is a permutation of a group's 16 pages.
All inputs are finite; a program needn't handle non-finite values.
Results may differ from the reference program's by a relative error of at most 0.017.
Values may be sent and summed in bfloat16 or wider, within the bound.
A program may use at most 192 MiB of HBM per device.

```python
import math
import jax
import jax.numpy as jnp
import numpy as np
from jax import lax

MODEL_DIM = 5120
HD = 128
TXT = 512
H = 32
FF = 8192
ADAPTER_RANK = 16
RQ = 4
PAGE = 16
GT = 256
QUERY_HEAD_WIDTH = 4096
LONGEST = 160
TOKENS = 1024
REQS = 16
ADAPTER_TOTAL = 32
PAGES_G = 16
N_REQ = 4


def with_ends(drawn, own_key, low, top_value):
    spot = [jax.random.randint(jax.random.fold_in(own_key, axis), (), 0, length) for axis, length in enumerate(drawn.shape)]
    widest = drawn.shape.index(max(drawn.shape))
    beside = spot[:widest] + [(spot[widest] + 1) % drawn.shape[widest]] + spot[widest + 1:]
    return drawn.at[tuple(spot)].set(low).at[tuple(beside)].set(top_value)


def steps_of(stream_key, dims, shards, least, top_value):
    gain, own = 1.0, jax.random.fold_in(stream_key, 6)
    for dim, parts in shards:
        heights = jnp.exp(jax.random.uniform(jax.random.fold_in(own, dim), (parts,), jnp.float32, least / len(shards), top_value / len(shards)))
        gain = gain * jnp.repeat(heights, dims[dim] // parts).reshape([-1 if axis == dim else 1 for axis in range(len(dims))])
    return gain


def split_up(amount, total, reach, slope):
    loads = [(1 << 20) // math.isqrt(rank ** slope) + 1 for rank in range(2, amount + 1)]
    surplus, given = total - reach - (amount - 1), [1] * (amount - 1)
    while surplus > 0:
        free = [i for i in range(amount - 1) if given[i] < reach]
        mass, left = sum([loads[i] for i in free]), surplus
        for i in free:
            addition = min(reach - given[i], max(1, left * loads[i] // mass), surplus)
            given[i] = given[i] + addition
            surplus = surplus - addition
    return np.array([reach] + given)


def uneven_parts(key, amount, total, bound, skew):
    if amount == 2:
        one = jax.random.randint(key, (), max(1, total - bound), min(bound, total - 1) + 1)
        return jnp.stack([one, total - one])
    sizes = jnp.asarray(split_up(amount, total, bound, skew), jnp.int32)
    twos = (amount - 1) // 2
    giver, taker = sizes[1:1 + 2 * twos:2], sizes[2:2 + 2 * twos:2]
    room = jnp.minimum(giver - 1, bound - taker)
    shifted = jax.random.randint(jax.random.fold_in(key, 1), (twos,), 0, 1 << 20) % (room + 1)
    sizes = sizes.at[1:1 + 2 * twos:2].set(giver - shifted).at[2:2 + 2 * twos:2].set(taker + shifted)
    return sizes[jax.random.permutation(jax.random.fold_in(key, 2), amount)]


def centred(stream_key, extent, scale, most, pieces=(), kind=jnp.bfloat16):
    entries = jax.random.normal(stream_key, extent, jnp.float32) * scale
    if len(pieces) > 0:
        entries = steps_of(stream_key, extent, pieces, -0.22, 0.18) * entries
    return jnp.clip(entries, min=-most, max=most).astype(kind)


def setup_inputs(seed: int = 0) -> dict:
    key_of = jax.random.split(jax.random.key(seed), 17)
    return {
        "tokens": centred(key_of[0], (TOKENS, MODEL_DIM), 1.0, 6.0, ((0, 32),)),
        "modulation": centred(key_of[1], (REQS, 6, MODEL_DIM), 0.5, 3.0, ((0, 4),), jnp.float32),
        "lengths": jax.vmap(lambda own: uneven_parts(own, RQ, GT, LONGEST, 2))(jax.random.split(key_of[2], N_REQ)).reshape((N_REQ, RQ)).astype(jnp.int32),
        "request_adapter": with_ends(jax.random.randint(key_of[3], (REQS,), 0, ADAPTER_TOTAL), jax.random.fold_in(key_of[3], 1), 0, ADAPTER_TOTAL - 1).astype(jnp.int32),
        "adapter_storage": jax.random.permutation(key_of[4], ADAPTER_TOTAL).astype(jnp.int32),
        "adapter_down_weight": centred(key_of[5], (ADAPTER_TOTAL, MODEL_DIM, 2 * ADAPTER_RANK), MODEL_DIM ** -0.5, 0.078125, ((0, 8),)),
        "adapter_up_maps": centred(key_of[6], (ADAPTER_TOTAL, 2, ADAPTER_RANK, QUERY_HEAD_WIDTH), ADAPTER_RANK ** -0.5, 1.5, ((0, 8),)),
        "input_projection": centred(key_of[7], (4, MODEL_DIM, QUERY_HEAD_WIDTH), MODEL_DIM ** -0.5, 0.078125, ((2, 8),)),
        "query_key_gains": jnp.clip(1.0 + 0.18 * jax.random.normal(key_of[8], (3, QUERY_HEAD_WIDTH), jnp.float32), 0.1, 1.9),
        "positions": with_ends(jax.random.randint(key_of[9], (3, TOKENS), 0, 64), jax.random.fold_in(key_of[9], 1), 0, 63).astype(jnp.int32),
        "block_page_lookup": jax.vmap(lambda own: jax.random.permutation(own, PAGES_G))(jax.random.split(key_of[10], N_REQ)).reshape((N_REQ, PAGES_G)).astype(jnp.int32),
        "output_projection": centred(key_of[11], (2, QUERY_HEAD_WIDTH, MODEL_DIM), QUERY_HEAD_WIDTH ** -0.5, 0.09375, ((1, 8),)),
        "cross_norm_gain": jnp.clip(1.0 + 0.18 * jax.random.normal(key_of[12], (MODEL_DIM,), jnp.float32), 0.1, 1.9),
        "text_token_cache": centred(key_of[13], (2, REQS, TXT, QUERY_HEAD_WIDTH), 1.0, 3.0, ((1, 4), (3, 8))),
        "feedforward_up": centred(key_of[14], (MODEL_DIM, FF), MODEL_DIM ** -0.5, 0.078125, ((0, 4), (1, 8))),
        "feedforward_down": centred(key_of[15], (FF, MODEL_DIM), FF ** -0.5, 0.0625, ((0, 8), (1, 4))),
    }


EPSILON = 1e-06

def layer_norm(values):
    center = values - lax.optimization_barrier(jnp.mean(values, axis=-1, keepdims=True))
    spread = lax.optimization_barrier(jnp.mean(center * center, axis=-1, keepdims=True))
    return center * lax.rsqrt(spread + EPSILON)

def rotary_tables(grid):
    half_dim = HD // 2
    spatial = half_dim // 3
    temporal = half_dim - 2 * spatial
    column = jnp.arange(half_dim, dtype=jnp.int32)
    which_axis = jnp.where(column < temporal, 0, jnp.where(column < temporal + spatial, 1, 2)).astype(jnp.int32)
    offset = jnp.where(which_axis == 0, 0, jnp.where(which_axis == 1, temporal, temporal + spatial)).astype(jnp.int32)
    span_size = jnp.where(which_axis == 0, temporal, spatial).astype(jnp.float32)
    frequency = jnp.exp(-(column - offset).astype(jnp.float32) / span_size * math.log(10000.0))
    coordinate = grid.astype(jnp.float32)[which_axis, :].T
    angles = coordinate * frequency[None, :]
    return (jnp.cos(angles), jnp.sin(angles))

def rotate(values, cosine, sine_part):
    half_dim = HD // 2
    front_half = values[..., :half_dim]
    back_half = values[..., half_dim:]
    cosine = cosine[:, None, :]
    sine_part = sine_part[:, None, :]
    return jnp.concatenate([front_half * cosine - back_half * sine_part, back_half * cosine + front_half * sine_part], axis=-1)

def attend(queries, key_rows, value_rows, allowed):
    scores = jnp.einsum('thd,shd->hts', queries.astype(jnp.float32), key_rows.astype(jnp.float32)) / math.sqrt(HD)
    scores = jnp.where(allowed[None], scores, -1e+30)
    weights = jnp.exp(scores)
    weights = (weights / lax.optimization_barrier(jnp.sum(weights, axis=-1, keepdims=True))).astype(jnp.bfloat16)
    return jnp.einsum('hts,shd->thd', weights.astype(jnp.float32), value_rows.astype(jnp.float32)).astype(jnp.bfloat16)

def reference(tokens, modulation, lengths, request_adapter, adapter_storage, adapter_down_weight, adapter_up_maps, input_projection, query_key_gains, positions, block_page_lookup, output_projection, cross_norm_gain, text_token_cache, feedforward_up, feedforward_down):
    entire_width = H * HD
    bounds = jnp.cumsum(lengths, axis=1)
    position = jnp.arange(GT, dtype=jnp.int32)
    segment = lax.optimization_barrier(jnp.sum((position[None, :, None] >= bounds[:, None, :]).astype(jnp.int32), axis=2))
    request = (jnp.arange(N_REQ, dtype=jnp.int32)[:, None] * RQ + segment).reshape(TOKENS)
    token_f32 = tokens.astype(jnp.float32)
    normed_in = (layer_norm(token_f32) * (1.0 + modulation[request, 1]) + modulation[request, 0]).astype(jnp.bfloat16)
    token_slot = adapter_storage[request_adapter[request]]
    down_combined = jnp.transpose(adapter_down_weight, (1, 0, 2)).reshape(MODEL_DIM, ADAPTER_TOTAL * 2 * ADAPTER_RANK)
    codes_all = jnp.dot(normed_in, down_combined, preferred_element_type=jnp.float32).reshape(TOKENS, ADAPTER_TOTAL, 2 * ADAPTER_RANK)
    everywhere = (token_slot[:, None] == jnp.arange(ADAPTER_TOTAL, dtype=jnp.int32)[None, :]).astype(jnp.float32)
    codes = lax.optimization_barrier(jnp.sum(everywhere[:, :, None] * codes_all, axis=1)).astype(jnp.bfloat16)

    def spread(code_part):
        return (everywhere[:, :, None] * code_part[:, None, :].astype(jnp.float32)).reshape(TOKENS, ADAPTER_TOTAL * ADAPTER_RANK).astype(jnp.bfloat16)
    query_up_weight = adapter_up_maps[:, 0].reshape(ADAPTER_TOTAL * ADAPTER_RANK, entire_width)
    value_up_weight = adapter_up_maps[:, 1].reshape(ADAPTER_TOTAL * ADAPTER_RANK, entire_width)
    query_linear = jnp.dot(normed_in, input_projection[0], preferred_element_type=jnp.float32) + jnp.dot(spread(codes[:, :ADAPTER_RANK]), query_up_weight, preferred_element_type=jnp.float32)
    key_linear = jnp.dot(normed_in, input_projection[1], preferred_element_type=jnp.float32)
    value_rows = (jnp.dot(normed_in, input_projection[2], preferred_element_type=jnp.float32) + jnp.dot(spread(codes[:, ADAPTER_RANK:]), value_up_weight, preferred_element_type=jnp.float32)).astype(jnp.bfloat16)
    query_norm = query_linear * lax.rsqrt(lax.optimization_barrier(jnp.mean(query_linear * query_linear, axis=1)) + EPSILON)[:, None] * query_key_gains[0]
    key_norm = key_linear * lax.rsqrt(lax.optimization_barrier(jnp.mean(key_linear * key_linear, axis=1)) + EPSILON)[:, None] * query_key_gains[1]
    cosine, sine_part = rotary_tables(positions)
    query_rot = rotate(query_norm.reshape(TOKENS, H, HD), cosine, sine_part).astype(jnp.bfloat16)
    key_rot = rotate(key_norm.reshape(TOKENS, H, HD), cosine, sine_part).astype(jnp.bfloat16)
    value_heads = value_rows.reshape(TOKENS, H, HD)
    stacked = jnp.stack([key_rot.reshape(N_REQ, PAGES_G, PAGE, entire_width), value_rows.reshape(N_REQ, PAGES_G, PAGE, entire_width)])
    group_index = jnp.arange(N_REQ, dtype=jnp.int32)[:, None]
    kv_pages = jnp.zeros_like(stacked).at[:, group_index, block_page_lookup].set(stacked).reshape(2, N_REQ * PAGES_G, PAGE, entire_width)
    attended_parts = []
    for group in range(N_REQ):
        rows_here = slice(group * GT, (group + 1) * GT)
        allowed = segment[group][:, None] == segment[group][None, :]
        attended_parts.append(attend(query_rot[rows_here], key_rot[rows_here], value_heads[rows_here], allowed).reshape(GT, entire_width))
    attended = jnp.concatenate(attended_parts, axis=0)
    first_res = (token_f32 + modulation[request, 2] * jnp.dot(attended, output_projection[0], preferred_element_type=jnp.float32)).astype(jnp.bfloat16)
    cross_in = (layer_norm(first_res.astype(jnp.float32)) * cross_norm_gain).astype(jnp.bfloat16)
    cross_linear = jnp.dot(cross_in, input_projection[3], preferred_element_type=jnp.float32)
    cross_query = (cross_linear * lax.rsqrt(lax.optimization_barrier(jnp.mean(cross_linear * cross_linear, axis=1)) + EPSILON)[:, None] * query_key_gains[2]).astype(jnp.bfloat16)
    text_owner = jnp.arange(RQ * TXT, dtype=jnp.int32) // TXT
    cross_parts = []
    for group in range(N_REQ):
        rows_here = slice(group * GT, (group + 1) * GT)
        text_keys = text_token_cache[0, group * RQ:(group + 1) * RQ].reshape(RQ * TXT, H, HD)
        text_values = text_token_cache[1, group * RQ:(group + 1) * RQ].reshape(RQ * TXT, H, HD)
        allowed = segment[group][:, None] == text_owner[None, :]
        cross_parts.append(attend(cross_query[rows_here].reshape(GT, H, HD), text_keys, text_values, allowed).reshape(GT, entire_width))
    cross_out = jnp.concatenate(cross_parts, axis=0)
    second_res = (first_res.astype(jnp.float32) + jnp.dot(cross_out, output_projection[1], preferred_element_type=jnp.float32)).astype(jnp.bfloat16)
    mlp_in = (layer_norm(second_res.astype(jnp.float32)) * (1.0 + modulation[request, 4]) + modulation[request, 3]).astype(jnp.bfloat16)
    hidden = jax.nn.gelu(jnp.dot(mlp_in, feedforward_up, preferred_element_type=jnp.float32), approximate=True).astype(jnp.bfloat16)
    layer_out = (second_res.astype(jnp.float32) + modulation[request, 5] * jnp.dot(hidden, feedforward_down, preferred_element_type=jnp.float32)).astype(jnp.bfloat16)
    return (layer_out, kv_pages)
```

```python
import functools
import math

import jax
import jax.numpy as jnp
from jax import lax
from jax.experimental import pallas as pl
from jax.experimental.pallas import tpu as pltpu
from jax.sharding import PartitionSpec as P

HD = 128
PAGE = 16


EPSILON = 1e-06


PAIR = 2
MESH = pl.DeviceIdType.MESH
ANY = pl.BlockSpec(memory_space=pl.ANY)
VM = pl.BlockSpec(memory_space=pltpu.VMEM)


def comm_call(kernel, out_shape, in_specs, out_specs, scratch, ident):
    return pl.pallas_call(
        kernel,
        out_shape=out_shape,
        in_specs=in_specs,
        out_specs=out_specs,
        scratch_shapes=scratch,
        compiler_params=pltpu.CompilerParams(
            collective_id=ident, has_side_effects=True, vmem_limit_bytes=48 << 20
        ),
    )


def remote(source, target, send_sem, recv_sem, axis, place):
    return pltpu.make_async_remote_copy(
        src_ref=source,
        dst_ref=target,
        send_sem=send_sem,
        recv_sem=recv_sem,
        device_id={axis: place},
        device_id_type=MESH,
    )


def shift(me, step, count):
    return lax.rem(me + (step + count) % count, count)


def greet(peers):
    barrier = pltpu.get_barrier_semaphore()
    for axis, place in peers:
        pl.semaphore_signal(barrier, inc=1, device_id={axis: place}, device_id_type=MESH)
    pl.semaphore_wait(barrier, len(peers))


def pair_places(count):
    me = lax.axis_index("mlp")
    outer, core = lax.div(me, PAIR), lax.rem(me, PAIR)
    sibling = outer * PAIR + (PAIR - 1 - core)
    peers = [
        shift(outer, k, count // PAIR) * PAIR + core for k in range(count // PAIR)
    ]
    sources = [
        shift(outer, -k, count // PAIR) * PAIR + core for k in range(count // PAIR)
    ]
    return me, core, sibling, peers, sources


def gather_sems(count):
    steps = count // PAIR
    return [pltpu.SemaphoreType.DMA(())] + [pltpu.SemaphoreType.DMA((steps,))] * 4


def gather_rows(count, places, own_ref, out_ref, own_sem, send_sem, recv_sem, pass_send, pass_recv):
    me, core, sibling, peers, sources = places
    own = pltpu.make_async_copy(own_ref, out_ref.at[me], own_sem)
    sends = [
        remote(own_ref, out_ref.at[me], send_sem.at[k], recv_sem.at[k], "mlp", peers[k])
        for k in range(1, count // PAIR)
    ]
    for copy in sends:
        copy.start()
    passes = [remote(own_ref, out_ref.at[me], pass_send.at[0], pass_recv.at[0], "mlp", sibling)]
    passes[0].start()
    own.start()
    for k in range(1, count // PAIR):
        sends[k - 1].wait_recv()
        block = out_ref.at[sources[k]]
        passes.append(remote(block, block, pass_send.at[k], pass_recv.at[k], "mlp", sibling))
        passes[-1].start()
    for copy in sends:
        copy.wait_send()
    for copy in passes:
        copy.wait()
    own.wait()


def entry_kernel(count, tok_ref, scale_ref, shift_ref, maps_ref, out_ref, up_ref, norm, map_own, map_send, map_recv, *sems):
    places = pair_places(count)
    me = places[0]
    slots, width = maps_ref.shape[0], up_ref.shape[-1]
    others = [shift(me, k, count) for k in range(1, count)]
    greet([("mlp", place) for place in others])

    def columns(place):
        return maps_ref.at[:, :, :, pl.ds(pl.multiple_of(place * width, 128), width)]

    target = up_ref.at[pl.ds(me * slots, slots)]
    own = pltpu.make_async_copy(columns(me), target, map_own)
    own.start()
    copies = [
        remote(columns(place), target, map_send.at[k], map_recv.at[k], "mlp", place)
        for k, place in enumerate(others)
    ]
    norm[...] = (
        layer_norm(tok_ref[...].astype(jnp.float32)) * (1.0 + scale_ref[...]) + shift_ref[...]
    ).astype(jnp.bfloat16)
    for copy in copies:
        copy.start()
    gather_rows(count, places, norm, out_ref, *sems)
    for copy in copies:
        copy.wait()
    own.wait()


def entry_rows(tokens, scale, shift_rows, maps, count):
    rows, width = tokens.shape
    slots, two, rank, total = maps.shape
    dma = pltpu.SemaphoreType.DMA
    gathered, up = comm_call(
        functools.partial(entry_kernel, count),
        (
            jax.ShapeDtypeStruct((count, rows, width), jnp.bfloat16),
            jax.ShapeDtypeStruct((count * slots, two, rank, total // count), maps.dtype),
        ),
        [VM, VM, VM, ANY],
        (ANY, ANY),
        [pltpu.VMEM((rows, width), jnp.bfloat16), dma(()), dma((count - 1,)), dma((count - 1,))]
        + gather_sems(count),
        0,
    )(tokens, scale, shift_rows, maps)
    return gathered.reshape(count * rows, width), up


def sum_blocks(count, places, block_of, near, mid, far, ns, nr, fs, fr):
    me, core, sibling, peers, sources = places
    steps = count // PAIR
    order = list(range(1, steps)) + [0]
    pairs = {}
    for k in order:
        other = peers[k] + (PAIR - 1 - 2 * core)
        pairs[k] = remote(block_of(other), near.at[k], ns.at[k], nr.at[k], "mlp", sibling)
        pairs[k].start()
    sends = []
    for k in range(1, steps):
        pairs[k].wait_recv()
        mid[k] = (
            block_of(peers[k])[...].astype(jnp.float32) + near[k].astype(jnp.float32)
        ).astype(jnp.bfloat16)
        sends.append(remote(mid.at[k], far.at[k], fs.at[k], fr.at[k], "mlp", peers[k]))
        sends[-1].start()
    pairs[0].wait_recv()
    total = block_of(me)[...].astype(jnp.float32) + near[0].astype(jnp.float32)
    for k in range(1, steps):
        sends[k - 1].wait_recv()
        total = total + far[k].astype(jnp.float32)
    for k in order:
        pairs[k].wait_send()
    for copy in sends:
        copy.wait_send()
    return total


def sum_scratch(count, extent):
    steps = count // PAIR
    return [pltpu.VMEM((steps,) + extent, jnp.bfloat16)] * 3 + [
        pltpu.SemaphoreType.DMA((steps,))
    ] * 4


def middle_kernel(count, part_ref, base_ref, gate_ref, scale_ref, shift_ref, res_ref, out_ref, near, mid, far, norm, ns, nr, fs, fr, *sems):
    places = pair_places(count)
    greet([("mlp", places[2])] + [("mlp", place) for place in places[3][1:]])
    total = sum_blocks(
        count, places, lambda place: part_ref.at[place], near, mid, far, ns, nr, fs, fr
    )
    res = (base_ref[...].astype(jnp.float32) + gate_ref[...] * total).astype(jnp.bfloat16)
    res_ref[...] = res
    norm[...] = (layer_norm(res.astype(jnp.float32)) * scale_ref[...] + shift_ref[...]).astype(
        jnp.bfloat16
    )
    gather_rows(count, places, norm, out_ref, *sems)


def middle_rows(part, base, gate, scale, shift_rows, count, ident):
    rows, width = base.shape
    scratch = sum_scratch(count, (rows, width))
    res, gathered = comm_call(
        functools.partial(middle_kernel, count),
        (
            jax.ShapeDtypeStruct((rows, width), jnp.bfloat16),
            jax.ShapeDtypeStruct((count, rows, width), jnp.bfloat16),
        ),
        [VM] * 5,
        (VM, ANY),
        scratch[:3] + [pltpu.VMEM((rows, width), jnp.bfloat16)] + scratch[3:] + gather_sems(count),
        ident,
    )(part.reshape(count, rows, width), base, gate, scale, shift_rows)
    return res, gathered.reshape(count * rows, width)


def small_kernel(count, own_ref, out_ref, slots, send_sem, recv_sem):
    me = lax.axis_index("mlp")
    others = [shift(me, k, count) for k in range(1, count)]
    greet([("mlp", place) for place in others])
    copies = [
        remote(own_ref, slots.at[k], send_sem.at[k], recv_sem.at[k], "mlp", place)
        for k, place in enumerate(others)
    ]
    for copy in copies:
        copy.start()
    total = own_ref[...].astype(jnp.float32)
    for k, copy in enumerate(copies):
        copy.wait_recv()
        total = total + slots[k].astype(jnp.float32)
    out_ref[...] = total
    for copy in copies:
        copy.wait_send()


def small_sum(own, count, ident):
    dma = pltpu.SemaphoreType.DMA((count - 1,))
    return comm_call(
        functools.partial(small_kernel, count),
        jax.ShapeDtypeStruct(own.shape, jnp.float32),
        [VM],
        VM,
        [pltpu.VMEM((count - 1,) + own.shape, own.dtype), dma, dma],
        ident,
    )(own)


def line_kernel(count, own_ref, out_ref, own_sem, rs, rr, ls, lr):
    me = lax.axis_index("req")
    right, left = shift(me, 1, count), shift(me, -1, count)
    greet([("req", right), ("req", left)])
    own = pltpu.make_async_copy(own_ref, out_ref.at[me], own_sem)
    own.start()

    def hop(step, sign):
        block = jnp.clip(me - sign * step, 0, count - 1)
        source = own_ref if step == 0 else out_ref.at[block]
        send, recv, place = (rs, rr, right) if sign > 0 else (ls, lr, left)
        return remote(source, out_ref.at[block], send.at[step], recv.at[step], "req", place)

    for step in range(count - 1):
        if step > 0:

            @pl.when(me >= step)
            def _():
                hop(step - 1, 1).wait_recv()

            @pl.when(me + step < count)
            def _():
                hop(step - 1, -1).wait_recv()

        @pl.when((me >= step) & (me < count - 1))
        def _():
            hop(step, 1).start()

        @pl.when((me + step < count) & (me > 0))
        def _():
            hop(step, -1).start()

    @pl.when(me >= count - 1)
    def _():
        hop(count - 2, 1).wait_recv()

    @pl.when(me < 1)
    def _():
        hop(count - 2, -1).wait_recv()

    for step in range(count - 1):

        @pl.when((me >= step) & (me < count - 1))
        def _():
            hop(step, 1).wait_send()

        @pl.when((me + step < count) & (me > 0))
        def _():
            hop(step, -1).wait_send()

    own.wait()


def line_gather(own, count, ident):
    dma = pltpu.SemaphoreType.DMA
    return comm_call(
        functools.partial(line_kernel, count),
        jax.ShapeDtypeStruct((count,) + own.shape, own.dtype),
        [ANY],
        ANY,
        [dma(())] + [dma((count - 1,))] * 4,
        ident,
    )(own)


def exit_kernel(count, lines, part_ref, out_ref, near, mid, far, final, ns, nr, fs, fr, own_sem, send_sem, recv_sem):
    places = pair_places(count)
    line = lax.axis_index("req")
    others = [shift(line, k, lines) for k in range(1, lines)]
    greet(
        [("mlp", places[2])]
        + [("mlp", place) for place in places[3][1:]]
        + [("req", place) for place in others]
    )
    final[...] = sum_blocks(
        count, places, lambda place: part_ref.at[:, place], near, mid, far, ns, nr, fs, fr
    ).astype(jnp.bfloat16)
    width = final.shape[-1]
    target = out_ref.at[:, pl.ds(pl.multiple_of(line * width, 128), width)]
    own = pltpu.make_async_copy(final.at[line], target, own_sem)
    own.start()
    copies = [
        remote(final.at[place], target, send_sem.at[k], recv_sem.at[k], "req", place)
        for k, place in enumerate(others)
    ]
    for copy in copies:
        copy.start()
    for copy in copies:
        copy.wait()
    own.wait()


def exit_rows(part, count, lines, ident):
    groups, _, rows, width = part.shape
    scratch = sum_scratch(count, (groups, rows, width))
    dma = pltpu.SemaphoreType.DMA
    return comm_call(
        functools.partial(exit_kernel, count, lines),
        jax.ShapeDtypeStruct((rows, lines * width), jnp.bfloat16),
        [VM],
        VM,
        scratch[:3]
        + [pltpu.VMEM((groups, rows, width), jnp.bfloat16)]
        + scratch[3:]
        + [dma(()), dma((lines - 1,)), dma((lines - 1,))],
        ident,
    )(part)


def layer_norm(values):
    center = values - jnp.mean(values, axis=-1, keepdims=True)
    spread = jnp.mean(center * center, axis=-1, keepdims=True)
    return center * lax.rsqrt(spread + EPSILON)


def rotary_tables(grid):
    half_dim = HD // 2
    spatial = half_dim // 3
    temporal = half_dim - 2 * spatial
    column = jnp.arange(half_dim, dtype=jnp.int32)
    which_axis = jnp.where(
        column < temporal, 0, jnp.where(column < temporal + spatial, 1, 2)
    ).astype(jnp.int32)
    offset = jnp.where(
        which_axis == 0, 0, jnp.where(which_axis == 1, temporal, temporal + spatial)
    ).astype(jnp.int32)
    span_size = jnp.where(which_axis == 0, temporal, spatial).astype(jnp.float32)
    frequency = jnp.exp(-(column - offset).astype(jnp.float32) / span_size * math.log(10000.0))
    coordinate = grid.astype(jnp.float32)[which_axis, :].T
    angles = coordinate * frequency[None, :]
    return (jnp.cos(angles), jnp.sin(angles))


def rotate(values, cosine, sine_part):
    half_dim = HD // 2
    front_half = values[..., :half_dim]
    back_half = values[..., half_dim:]
    cosine = cosine[:, None, :]
    sine_part = sine_part[:, None, :]
    return jnp.concatenate(
        [front_half * cosine - back_half * sine_part, back_half * cosine + front_half * sine_part],
        axis=-1,
    )


def attend(queries, key_rows, value_rows, allowed):
    scores = jnp.einsum(
        "thd,shd->hts", queries, key_rows, preferred_element_type=jnp.float32
    ) / math.sqrt(HD)
    scores = jnp.where(allowed[None], scores, -1e30)
    weights = jnp.exp(scores)
    weights = (weights / jnp.sum(weights, axis=-1, keepdims=True)).astype(jnp.bfloat16)
    return jnp.einsum(
        "hts,shd->thd", weights, value_rows, preferred_element_type=jnp.float32
    ).astype(jnp.bfloat16)


def choose_rows(table, segment):
    chosen = jnp.zeros((segment.shape[0],) + table.shape[1:], table.dtype)
    for request in range(table.shape[0]):
        picked = (segment == request).reshape((-1,) + (1,) * (table.ndim - 1))
        chosen = jnp.where(picked, table[request][None], chosen)
    return chosen


def body(
    tokens,
    modulation,
    lengths,
    request_adapter,
    adapter_storage,
    adapter_down_weight,
    adapter_up_maps,
    input_projection,
    query_key_gains,
    positions,
    block_page_lookup,
    output_projection,
    cross_norm_gain,
    text_token_cache,
    feedforward_up,
    feedforward_down,
):
    mlp_count = lax.axis_size("mlp")
    my_index = lax.axis_index("mlp")
    own_count = tokens.shape[0]
    group_rows = own_count * mlp_count
    local_width = input_projection.shape[2]
    heads_local = local_width // HD
    entire_width = local_width * mlp_count
    resident_slots = adapter_down_weight.shape[0]
    doubled_rank = adapter_down_weight.shape[2]
    rank_once = doubled_rank // 2

    req_count = lax.axis_size("req")
    slot_total = resident_slots * mlp_count
    up_full = lax.all_gather(feedforward_up, "req", axis=0, tiled=True)
    bounds = jnp.cumsum(lengths[0])
    position = jnp.arange(group_rows, dtype=jnp.int32)
    segment = jnp.sum((position[:, None] >= bounds[None, :]).astype(jnp.int32), axis=1)
    own_start = my_index * own_count
    own_segment = lax.dynamic_slice_in_dim(segment, own_start, own_count)
    per_token = [choose_rows(modulation[:, which_row, :], own_segment) for which_row in range(6)]
    token_f32 = tokens.astype(jnp.float32)
    rows_in, adapter_up_weight = entry_rows(
        tokens, per_token[1], per_token[0], adapter_up_maps, mlp_count
    )
    request_slot = adapter_storage[request_adapter]
    token_slot = choose_rows(request_slot, segment)
    resident = my_index * resident_slots + jnp.arange(resident_slots, dtype=jnp.int32)
    held = (token_slot[None, :] == resident[:, None]).astype(jnp.float32)
    code_block = lax.dot_general(
        adapter_down_weight.transpose(0, 2, 1).reshape(resident_slots * doubled_rank, -1),
        rows_in,
        (((1,), (1,)), ((), ())),
        preferred_element_type=jnp.float32,
    ).reshape(resident_slots, doubled_rank, group_rows)
    my_codes = jnp.sum(held[:, None, :] * code_block, axis=0).astype(jnp.bfloat16)
    codes = small_sum(my_codes, mlp_count, 1).astype(jnp.bfloat16)
    slots = jnp.arange(slot_total, dtype=jnp.int32)
    everywhere = token_slot[None, :] == slots[:, None]

    def spread(code_part):
        return jnp.where(everywhere[:, None, :], code_part[None], jnp.bfloat16(0)).reshape(
            slot_total * rank_once, group_rows
        )

    def adapted(code_part, which_map):
        return lax.dot_general(
            spread(code_part),
            adapter_up_weight[:, which_map].reshape(slot_total * rank_once, local_width),
            (((0,), (0,)), ((), ())),
            preferred_element_type=jnp.float32,
        )

    def project(which_map):
        return jnp.dot(rows_in, input_projection[which_map], preferred_element_type=jnp.float32)

    query_linear = project(0) + adapted(codes[:rank_once], 0)
    key_linear = project(1)
    value_rows = (project(2) + adapted(codes[rank_once:], 1)).astype(jnp.bfloat16)
    squares = small_sum(
        jnp.stack(
            [jnp.sum(query_linear * query_linear, axis=1), jnp.sum(key_linear * key_linear, axis=1)]
        ),
        mlp_count,
        2,
    )
    query_square, key_square = squares[0], squares[1]
    query_norm = (
        query_linear
        * lax.rsqrt(query_square / entire_width + EPSILON)[:, None]
        * query_key_gains[0]
    )
    key_norm = (
        key_linear * lax.rsqrt(key_square / entire_width + EPSILON)[:, None] * query_key_gains[1]
    )
    cosine, sine_part = rotary_tables(positions)
    query_rot = rotate(query_norm.reshape(group_rows, heads_local, HD), cosine, sine_part).astype(
        jnp.bfloat16
    )
    key_rot = rotate(key_norm.reshape(group_rows, heads_local, HD), cosine, sine_part).astype(
        jnp.bfloat16
    )
    value_heads = value_rows.reshape(group_rows, heads_local, HD)
    page_count = group_rows // PAGE
    stacked = jnp.stack(
        [
            key_rot.reshape(page_count, PAGE, local_width),
            value_rows.reshape(page_count, PAGE, local_width),
        ]
    )
    kv_pages = jnp.zeros_like(stacked).at[:, block_page_lookup[0]].set(stacked)
    allowed = segment[:, None] == segment[None, :]
    attended = attend(query_rot, key_rot, value_heads, allowed).reshape(group_rows, local_width)
    text_owner = (
        jnp.arange(text_token_cache.shape[1] * text_token_cache.shape[2], dtype=jnp.int32)
        // text_token_cache.shape[2]
    )
    cross_allowed = segment[:, None] == text_owner[None, :]
    text_keys = text_token_cache[0].reshape(-1, heads_local, HD)
    text_values = text_token_cache[1].reshape(-1, heads_local, HD)

    def out_rows(rows, which_map):
        return jnp.dot(
            rows, output_projection[which_map], preferred_element_type=jnp.float32
        ).astype(jnp.bfloat16)

    first_res, cross_in = middle_rows(
        out_rows(attended, 0),
        tokens,
        per_token[2],
        cross_norm_gain[None, :],
        jnp.zeros((1, tokens.shape[1]), jnp.float32),
        mlp_count,
        3,
    )
    cross_linear = jnp.dot(cross_in, input_projection[3], preferred_element_type=jnp.float32)
    cross_square = small_sum(
        jnp.sum(cross_linear * cross_linear, axis=1)[None, :], mlp_count, 4
    )[0]
    cross_query = (
        cross_linear
        * lax.rsqrt(cross_square / entire_width + EPSILON)[:, None]
        * query_key_gains[2]
    ).astype(jnp.bfloat16)
    cross_out = attend(
        cross_query.reshape(group_rows, heads_local, HD), text_keys, text_values, cross_allowed
    ).reshape(group_rows, local_width)

    second_res, mlp_in = middle_rows(
        out_rows(cross_out, 1),
        first_res,
        jnp.ones((1, tokens.shape[1]), jnp.float32),
        1.0 + per_token[4],
        per_token[3],
        mlp_count,
        5,
    )
    hidden = jax.nn.gelu(
        jnp.dot(mlp_in, up_full, preferred_element_type=jnp.float32), approximate=True
    ).astype(jnp.bfloat16)
    hidden_all = line_gather(hidden, req_count, 6)
    units, columns = feedforward_down.shape
    down_part = jnp.dot(
        hidden_all.reshape(req_count * group_rows, units),
        feedforward_down,
        preferred_element_type=jnp.float32,
    ).astype(jnp.bfloat16)
    down_own = exit_rows(
        down_part.reshape(req_count, mlp_count, own_count, columns), mlp_count, req_count, 7
    )
    layer_out = (
        second_res.astype(jnp.float32) + per_token[5] * down_own.astype(jnp.float32)
    ).astype(jnp.bfloat16)
    return (layer_out, kv_pages)


def solution(mesh):
    return jax.shard_map(
        body,
        mesh=mesh,
        in_specs=(
            P(("req", "mlp"), None),
            P("req", None, None),
            P("req", None),
            P("req"),
            P(),
            P("mlp", None, None),
            P("mlp", None, None, None),
            P(None, None, "mlp"),
            P(None, "mlp"),
            P(None, "req"),
            P("req", None),
            P(None, "mlp", None),
            P(),
            P(None, "req", None, "mlp"),
            P("req", "mlp"),
            P("mlp", "req"),
        ),
        out_specs=(P(("req", "mlp"), None), P(None, "req", None, "mlp")),
        check_vma=False,
    )
```

```python
import functools
import math

import jax
import jax.numpy as jnp
from jax import lax
from jax.experimental import pallas as pl
from jax.experimental.pallas import tpu as pltpu
from jax.sharding import PartitionSpec as P

HD = 128
PAGE = 16


EPSILON = 1e-06


PAIR = 2
MESH = pl.DeviceIdType.MESH
ANY = pl.BlockSpec(memory_space=pl.ANY)
VM = pl.BlockSpec(memory_space=pltpu.VMEM)


def comm_call(kernel, out_shape, in_specs, out_specs, scratch, ident, room=4):
    return pl.pallas_call(
        kernel,
        out_shape=out_shape,
        in_specs=in_specs,
        out_specs=out_specs,
        scratch_shapes=scratch,
        compiler_params=pltpu.CompilerParams(
            collective_id=ident, has_side_effects=True, vmem_limit_bytes=room << 20
        ),
    )


def remote(source, target, send_sem, recv_sem, axis, place):
    return pltpu.make_async_remote_copy(
        src_ref=source,
        dst_ref=target,
        send_sem=send_sem,
        recv_sem=recv_sem,
        device_id={axis: place},
        device_id_type=MESH,
    )


def shift(me, step, count):
    return lax.rem(me + (step + count) % count, count)


def greet(peers):
    barrier = pltpu.get_barrier_semaphore()
    for axis, place in peers:
        pl.semaphore_signal(barrier, inc=1, device_id={axis: place}, device_id_type=MESH)
    pl.semaphore_wait(barrier, len(peers))


def pair_places(count):
    me = lax.axis_index("mlp")
    outer, core = lax.div(me, PAIR), lax.rem(me, PAIR)
    sibling = outer * PAIR + (PAIR - 1 - core)
    peers = [
        shift(outer, k, count // PAIR) * PAIR + core for k in range(count // PAIR)
    ]
    sources = [
        shift(outer, -k, count // PAIR) * PAIR + core for k in range(count // PAIR)
    ]
    return me, core, sibling, peers, sources


def gather_sems(count):
    steps = count // PAIR
    return [pltpu.SemaphoreType.DMA(())] + [pltpu.SemaphoreType.DMA((steps,))] * 4


def gather_rows(count, places, own_ref, out_ref, own_sem, send_sem, recv_sem, pass_send, pass_recv):
    me, core, sibling, peers, sources = places
    own = pltpu.make_async_copy(own_ref, out_ref.at[me], own_sem)
    sends = [
        remote(own_ref, out_ref.at[me], send_sem.at[k], recv_sem.at[k], "mlp", peers[k])
        for k in range(1, count // PAIR)
    ]
    for copy in sends:
        copy.start()
    passes = [remote(own_ref, out_ref.at[me], pass_send.at[0], pass_recv.at[0], "mlp", sibling)]
    passes[0].start()
    own.start()
    for k in range(1, count // PAIR):
        sends[k - 1].wait_recv()
        block = out_ref.at[sources[k]]
        passes.append(remote(block, block, pass_send.at[k], pass_recv.at[k], "mlp", sibling))
        passes[-1].start()
    for copy in sends:
        copy.wait_send()
    for copy in passes:
        copy.wait()
    own.wait()


def entry_kernel(count, tok_ref, scale_ref, shift_ref, maps_ref, out_ref, up_ref, norm, map_own, map_send, map_recv, *sems):
    places = pair_places(count)
    me = places[0]
    slots, width = maps_ref.shape[0], up_ref.shape[-1]
    others = [shift(me, k, count) for k in range(1, count)]
    greet([("mlp", place) for place in others])

    def columns(place):
        return maps_ref.at[:, :, :, pl.ds(pl.multiple_of(place * width, 128), width)]

    target = up_ref.at[pl.ds(me * slots, slots)]
    own = pltpu.make_async_copy(columns(me), target, map_own)
    own.start()
    copies = [
        remote(columns(place), target, map_send.at[k], map_recv.at[k], "mlp", place)
        for k, place in enumerate(others)
    ]
    norm[...] = (
        layer_norm(tok_ref[...].astype(jnp.float32)) * (1.0 + scale_ref[...]) + shift_ref[...]
    ).astype(jnp.bfloat16)
    for copy in copies:
        copy.start()
    gather_rows(count, places, norm, out_ref, *sems)
    for copy in copies:
        copy.wait()
    own.wait()


def entry_rows(tokens, scale, shift_rows, maps, count):
    rows, width = tokens.shape
    slots, two, rank, total = maps.shape
    dma = pltpu.SemaphoreType.DMA
    gathered, up = comm_call(
        functools.partial(entry_kernel, count),
        (
            jax.ShapeDtypeStruct((count, rows, width), jnp.bfloat16),
            jax.ShapeDtypeStruct((count * slots, two, rank, total // count), maps.dtype),
        ),
        [VM, VM, VM, ANY],
        (ANY, ANY),
        [pltpu.VMEM((rows, width), jnp.bfloat16), dma(()), dma((count - 1,)), dma((count - 1,))]
        + gather_sems(count),
        0,
        8,
    )(tokens, scale, shift_rows, maps)
    return gathered.reshape(count * rows, width), up


def sum_blocks(count, places, block_of, near, mid, far, ns, nr, fs, fr):
    me, core, sibling, peers, sources = places
    steps = count // PAIR
    order = list(range(1, steps)) + [0]
    pairs = {}
    for k in order:
        other = peers[k] + (PAIR - 1 - 2 * core)
        pairs[k] = remote(block_of(other), near.at[k], ns.at[k], nr.at[k], "mlp", sibling)
        pairs[k].start()
    sends = []
    for k in range(1, steps):
        pairs[k].wait_recv()
        mid[k] = (
            block_of(peers[k])[...].astype(jnp.float32) + near[k].astype(jnp.float32)
        ).astype(jnp.bfloat16)
        sends.append(remote(mid.at[k], far.at[k], fs.at[k], fr.at[k], "mlp", peers[k]))
        sends[-1].start()
    pairs[0].wait_recv()
    total = block_of(me)[...].astype(jnp.float32) + near[0].astype(jnp.float32)
    for k in range(1, steps):
        sends[k - 1].wait_recv()
        total = total + far[k].astype(jnp.float32)
    for k in order:
        pairs[k].wait_send()
    for copy in sends:
        copy.wait_send()
    return total


def sum_scratch(count, extent):
    steps = count // PAIR
    return [pltpu.VMEM((steps,) + extent, jnp.bfloat16)] * 3 + [
        pltpu.SemaphoreType.DMA((steps,))
    ] * 4


def middle_kernel(count, part_ref, base_ref, gate_ref, scale_ref, shift_ref, res_ref, out_ref, near, mid, far, norm, ns, nr, fs, fr, *sems):
    places = pair_places(count)
    greet([("mlp", places[2])] + [("mlp", place) for place in places[3][1:]])
    total = sum_blocks(
        count, places, lambda place: part_ref.at[place], near, mid, far, ns, nr, fs, fr
    )
    res = (base_ref[...].astype(jnp.float32) + gate_ref[...] * total).astype(jnp.bfloat16)
    res_ref[...] = res
    norm[...] = (layer_norm(res.astype(jnp.float32)) * scale_ref[...] + shift_ref[...]).astype(
        jnp.bfloat16
    )
    gather_rows(count, places, norm, out_ref, *sems)


def middle_rows(part, base, gate, scale, shift_rows, count, ident):
    rows, width = base.shape
    scratch = sum_scratch(count, (rows, width))
    res, gathered = comm_call(
        functools.partial(middle_kernel, count),
        (
            jax.ShapeDtypeStruct((rows, width), jnp.bfloat16),
            jax.ShapeDtypeStruct((count, rows, width), jnp.bfloat16),
        ),
        [VM] * 5,
        (VM, ANY),
        scratch[:3] + [pltpu.VMEM((rows, width), jnp.bfloat16)] + scratch[3:] + gather_sems(count),
        ident,
        24,
    )(part.reshape(count, rows, width), base, gate, scale, shift_rows)
    return res, gathered.reshape(count * rows, width)


def small_kernel(count, own_ref, out_ref, slots, send_sem, recv_sem):
    me = lax.axis_index("mlp")
    others = [shift(me, k, count) for k in range(1, count)]
    greet([("mlp", place) for place in others])
    copies = [
        remote(own_ref, slots.at[k], send_sem.at[k], recv_sem.at[k], "mlp", place)
        for k, place in enumerate(others)
    ]
    for copy in copies:
        copy.start()
    total = own_ref[...].astype(jnp.float32)
    for k, copy in enumerate(copies):
        copy.wait_recv()
        total = total + slots[k].astype(jnp.float32)
    out_ref[...] = total
    for copy in copies:
        copy.wait_send()


def small_sum(own, count, ident):
    dma = pltpu.SemaphoreType.DMA((count - 1,))
    return comm_call(
        functools.partial(small_kernel, count),
        jax.ShapeDtypeStruct(own.shape, jnp.float32),
        [VM],
        VM,
        [pltpu.VMEM((count - 1,) + own.shape, own.dtype), dma, dma],
        ident,
    )(own)


def line_kernel(count, own_ref, out_ref, own_sem, rs, rr, ls, lr):
    me = lax.axis_index("req")
    right, left = shift(me, 1, count), shift(me, -1, count)
    greet([("req", right), ("req", left)])
    own = pltpu.make_async_copy(own_ref, out_ref.at[me], own_sem)
    own.start()

    def hop(step, sign):
        block = jnp.clip(me - sign * step, 0, count - 1)
        source = own_ref if step == 0 else out_ref.at[block]
        send, recv, place = (rs, rr, right) if sign > 0 else (ls, lr, left)
        return remote(source, out_ref.at[block], send.at[step], recv.at[step], "req", place)

    for step in range(count - 1):
        if step > 0:

            @pl.when(me >= step)
            def _():
                hop(step - 1, 1).wait_recv()

            @pl.when(me + step < count)
            def _():
                hop(step - 1, -1).wait_recv()

        @pl.when((me >= step) & (me < count - 1))
        def _():
            hop(step, 1).start()

        @pl.when((me + step < count) & (me > 0))
        def _():
            hop(step, -1).start()

    @pl.when(me >= count - 1)
    def _():
        hop(count - 2, 1).wait_recv()

    @pl.when(me < 1)
    def _():
        hop(count - 2, -1).wait_recv()

    for step in range(count - 1):

        @pl.when((me >= step) & (me < count - 1))
        def _():
            hop(step, 1).wait_send()

        @pl.when((me + step < count) & (me > 0))
        def _():
            hop(step, -1).wait_send()

    own.wait()


def line_gather(own, count, ident):
    dma = pltpu.SemaphoreType.DMA
    return comm_call(
        functools.partial(line_kernel, count),
        jax.ShapeDtypeStruct((count,) + own.shape, own.dtype),
        [ANY],
        ANY,
        [dma(())] + [dma((count - 1,))] * 4,
        ident,
    )(own)


def exit_kernel(count, lines, part_ref, out_ref, near, mid, far, final, ns, nr, fs, fr, own_sem, send_sem, recv_sem):
    places = pair_places(count)
    line = lax.axis_index("req")
    others = [shift(line, k, lines) for k in range(1, lines)]
    greet(
        [("mlp", places[2])]
        + [("mlp", place) for place in places[3][1:]]
        + [("req", place) for place in others]
    )
    final[...] = sum_blocks(
        count, places, lambda place: part_ref.at[:, place], near, mid, far, ns, nr, fs, fr
    ).astype(jnp.bfloat16)
    width = final.shape[-1]
    target = out_ref.at[:, pl.ds(pl.multiple_of(line * width, 128), width)]
    own = pltpu.make_async_copy(final.at[line], target, own_sem)
    own.start()
    copies = [
        remote(final.at[place], target, send_sem.at[k], recv_sem.at[k], "req", place)
        for k, place in enumerate(others)
    ]
    for copy in copies:
        copy.start()
    for copy in copies:
        copy.wait()
    own.wait()


def exit_rows(part, count, lines, ident):
    groups, _, rows, width = part.shape
    scratch = sum_scratch(count, (groups, rows, width))
    dma = pltpu.SemaphoreType.DMA
    return comm_call(
        functools.partial(exit_kernel, count, lines),
        jax.ShapeDtypeStruct((rows, lines * width), jnp.bfloat16),
        [VM],
        VM,
        scratch[:3]
        + [pltpu.VMEM((groups, rows, width), jnp.bfloat16)]
        + scratch[3:]
        + [dma(()), dma((lines - 1,)), dma((lines - 1,))],
        ident,
        24,
    )(part)


def layer_norm(values):
    center = values - jnp.mean(values, axis=-1, keepdims=True)
    spread = jnp.mean(center * center, axis=-1, keepdims=True)
    return center * lax.rsqrt(spread + EPSILON)


def rotary_tables(grid):
    half_dim = HD // 2
    spatial = half_dim // 3
    temporal = half_dim - 2 * spatial
    column = jnp.arange(HD, dtype=jnp.int32)
    sign = jnp.where(column < half_dim, -1.0, 1.0).astype(jnp.float32)
    column = column % half_dim
    which_axis = jnp.where(
        column < temporal, 0, jnp.where(column < temporal + spatial, 1, 2)
    ).astype(jnp.int32)
    offset = jnp.where(
        which_axis == 0, 0, jnp.where(which_axis == 1, temporal, temporal + spatial)
    ).astype(jnp.int32)
    span_size = jnp.where(which_axis == 0, temporal, spatial).astype(jnp.float32)
    frequency = jnp.exp(-(column - offset).astype(jnp.float32) / span_size * math.log(10000.0))
    grid = grid.astype(jnp.float32)[:, :, None]
    coordinate = jnp.where(
        which_axis == 0, grid[0], jnp.where(which_axis == 1, grid[1], grid[2])
    )
    angles = coordinate * frequency[None, :]
    return (jnp.cos(angles), jnp.sin(angles) * sign[None, :])


def attend(queries, key_rows, value_rows, allowed):
    scores = lax.dot_general(
        queries, key_rows, (((1,), (1,)), ((), ())), preferred_element_type=jnp.float32
    ) * (1.0 / math.sqrt(HD))
    weights = jnp.exp(jnp.where(allowed, scores, -1e30))
    weights = weights * (1.0 / jnp.sum(weights, axis=-1, keepdims=True))
    return jnp.dot(
        weights.astype(jnp.bfloat16), value_rows, preferred_element_type=jnp.float32
    ).astype(jnp.bfloat16)


def self_kernel(page_ref, q_ref, k_ref, v_ref, qs_ref, ks_ref, gain_ref, cos_ref, sin_ref, seg_ref, segs_ref, out_ref, kv_ref):
    cosine, sine = cos_ref[...], sin_ref[...]
    allowed = seg_ref[...] == segs_ref[...]

    def turned(ref, scale, gain, columns):
        rows = ref[:, columns] * scale * gain_ref[gain : gain + 1, columns]
        return (rows * cosine + pltpu.roll(rows, HD // 2, 1) * sine).astype(jnp.bfloat16)

    for head in range(q_ref.shape[1] // HD):
        columns = slice(head * HD, (head + 1) * HD)
        query = turned(q_ref, qs_ref[...], 0, columns)
        key = turned(k_ref, ks_ref[...], 1, columns)
        value = v_ref[:, columns]
        out_ref[:, columns] = attend(query, key, value, allowed)
        for block in range(kv_ref.shape[1]):
            page = page_ref[block]
            rows = slice(block * PAGE, (block + 1) * PAGE)
            kv_ref[0, page, :, columns] = key[rows]
            kv_ref[1, page, :, columns] = value[rows]


def self_attention(pages, query, key, value, query_scale, key_scale, gains, cosine, sine, segment):
    rows, width = query.shape
    return pl.pallas_call(
        self_kernel,
        out_shape=(
            jax.ShapeDtypeStruct((rows, width), jnp.bfloat16),
            jax.ShapeDtypeStruct((2, pages.shape[0], PAGE, width), jnp.bfloat16),
        ),
        in_specs=[pl.BlockSpec(memory_space=pltpu.SMEM)] + [VM] * 10,
        out_specs=(VM, VM),
        compiler_params=pltpu.CompilerParams(vmem_limit_bytes=16 << 20),
    )(
        pages,
        query,
        key,
        value,
        query_scale[:, None],
        key_scale[:, None],
        gains,
        cosine,
        sine,
        segment[:, None],
        segment[None, :],
    )


def cross_kernel(q_ref, k_ref, v_ref, seg_ref, owner_ref, out_ref):
    out_ref[...] = attend(q_ref[...], k_ref[0], v_ref[0], seg_ref[...] == owner_ref[...])


def cross_attention(query, cache, segment, owner):
    rows, width = query.shape
    texts = cache.shape[1]
    head = pl.BlockSpec((rows, HD), lambda h: (0, h))
    return pl.pallas_call(
        cross_kernel,
        out_shape=jax.ShapeDtypeStruct((rows, width), jnp.bfloat16),
        grid=(width // HD,),
        in_specs=[
            head,
            pl.BlockSpec((1, texts, HD), lambda h: (0, 0, h)),
            pl.BlockSpec((1, texts, HD), lambda h: (1, 0, h)),
            pl.BlockSpec((rows, 1), lambda h: (0, 0)),
            pl.BlockSpec((1, texts), lambda h: (0, 0)),
        ],
        out_specs=head,
        compiler_params=pltpu.CompilerParams(vmem_limit_bytes=24 << 20),
    )(query, cache, cache, segment[:, None], owner[None, :])


def product_kernel(act, x_ref, w_ref, out_ref):
    out_ref[0] = act(
        jnp.dot(x_ref[...], w_ref[0], preferred_element_type=jnp.float32)
    ).astype(out_ref.dtype)


def product(rows_in, maps, first, amount, tile, dtype, act=lambda part: part):
    rows, depth = rows_in.shape
    width = maps.shape[2]
    tile = min(tile, width)
    return pl.pallas_call(
        functools.partial(product_kernel, act),
        out_shape=jax.ShapeDtypeStruct((amount, rows, width), dtype),
        grid=(amount, width // tile),
        in_specs=[
            pl.BlockSpec((rows, depth), lambda i, j: (0, 0)),
            pl.BlockSpec((1, depth, tile), lambda i, j: (first + i, 0, j)),
        ],
        out_specs=pl.BlockSpec((1, rows, tile), lambda i, j: (i, 0, j)),
        compiler_params=pltpu.CompilerParams(vmem_limit_bytes=24 << 20),
    )(rows_in, maps)


def choose_rows(table, segment):
    chosen = jnp.zeros((segment.shape[0],) + table.shape[1:], table.dtype)
    for request in range(table.shape[0]):
        picked = (segment == request).reshape((-1,) + (1,) * (table.ndim - 1))
        chosen = jnp.where(picked, table[request][None], chosen)
    return chosen


def body(
    tokens,
    modulation,
    lengths,
    request_adapter,
    adapter_storage,
    adapter_down_weight,
    adapter_up_maps,
    input_projection,
    query_key_gains,
    positions,
    block_page_lookup,
    output_projection,
    cross_norm_gain,
    text_token_cache,
    feedforward_up,
    feedforward_down,
):
    mlp_count = lax.axis_size("mlp")
    my_index = lax.axis_index("mlp")
    own_count = tokens.shape[0]
    group_rows = own_count * mlp_count
    local_width = input_projection.shape[2]
    entire_width = local_width * mlp_count
    resident_slots = adapter_down_weight.shape[0]
    doubled_rank = adapter_down_weight.shape[2]
    rank_once = doubled_rank // 2

    req_count = lax.axis_size("req")
    slot_total = resident_slots * mlp_count
    up_full = lax.all_gather(feedforward_up, "req", axis=0, tiled=True)
    bounds = jnp.cumsum(lengths[0])
    position = jnp.arange(group_rows, dtype=jnp.int32)
    segment = jnp.sum((position[:, None] >= bounds[None, :]).astype(jnp.int32), axis=1)
    own_start = my_index * own_count
    own_segment = lax.dynamic_slice_in_dim(segment, own_start, own_count)
    per_token = [choose_rows(modulation[:, which_row, :], own_segment) for which_row in range(6)]
    token_f32 = tokens.astype(jnp.float32)
    rows_in, adapter_up_weight = entry_rows(
        tokens, per_token[1], per_token[0], adapter_up_maps, mlp_count
    )
    request_slot = adapter_storage[request_adapter]
    token_slot = jnp.sum(
        jnp.where(
            segment[:, None] == jnp.arange(request_slot.shape[0], dtype=jnp.int32)[None, :],
            request_slot[None, :],
            0,
        ),
        axis=1,
    )
    resident = my_index * resident_slots + jnp.arange(resident_slots, dtype=jnp.int32)
    held = (token_slot[None, :] == resident[:, None]).astype(jnp.float32)
    code_block = lax.dot_general(
        adapter_down_weight.transpose(0, 2, 1).reshape(resident_slots * doubled_rank, -1),
        rows_in,
        (((1,), (1,)), ((), ())),
        preferred_element_type=jnp.float32,
    ).reshape(resident_slots, doubled_rank, group_rows)
    my_codes = jnp.sum(held[:, None, :] * code_block, axis=0).astype(jnp.bfloat16)
    codes = small_sum(my_codes, mlp_count, 1).astype(jnp.bfloat16)
    slots = jnp.arange(slot_total, dtype=jnp.int32)
    everywhere = token_slot[None, :] == slots[:, None]

    def spread(code_part):
        return jnp.where(everywhere[:, None, :], code_part[None], jnp.bfloat16(0)).reshape(
            slot_total * rank_once, group_rows
        )

    def adapted(code_part, which_map):
        return lax.dot_general(
            spread(code_part),
            adapter_up_weight[:, which_map].reshape(slot_total * rank_once, local_width),
            (((0,), (0,)), ((), ())),
            preferred_element_type=jnp.float32,
        )

    projected = product(rows_in, input_projection, 0, 3, 256, jnp.float32)
    query_linear = projected[0] + adapted(codes[:rank_once], 0)
    key_linear = projected[1]
    value_rows = (projected[2] + adapted(codes[rank_once:], 1)).astype(jnp.bfloat16)
    squares = small_sum(
        jnp.stack(
            [jnp.sum(query_linear * query_linear, axis=1), jnp.sum(key_linear * key_linear, axis=1)]
        ),
        mlp_count,
        2,
    )
    query_square, key_square = squares[0], squares[1]
    cosine, sine = rotary_tables(positions)
    attended, kv_pages = self_attention(
        block_page_lookup[0],
        query_linear,
        key_linear,
        value_rows,
        lax.rsqrt(query_square / entire_width + EPSILON),
        lax.rsqrt(key_square / entire_width + EPSILON),
        query_key_gains,
        cosine,
        sine,
        segment,
    )
    text_owner = (
        jnp.arange(text_token_cache.shape[1] * text_token_cache.shape[2], dtype=jnp.int32)
        // text_token_cache.shape[2]
    )

    def out_rows(rows, which_map):
        return product(rows, output_projection, which_map, 1, 1280, jnp.bfloat16)[0]

    first_res, cross_in = middle_rows(
        out_rows(attended, 0),
        tokens,
        per_token[2],
        cross_norm_gain[None, :],
        jnp.zeros((1, tokens.shape[1]), jnp.float32),
        mlp_count,
        3,
    )
    cross_linear = product(cross_in, input_projection, 3, 1, 256, jnp.float32)[0]
    cross_square = small_sum(
        jnp.sum(cross_linear * cross_linear, axis=1)[None, :], mlp_count, 4
    )[0]
    cross_query = (
        cross_linear
        * lax.rsqrt(cross_square / entire_width + EPSILON)[:, None]
        * query_key_gains[2]
    ).astype(jnp.bfloat16)
    cross_out = cross_attention(
        cross_query,
        text_token_cache.reshape(2, text_owner.shape[0], local_width),
        segment,
        text_owner,
    )
    second_res, mlp_in = middle_rows(
        out_rows(cross_out, 1),
        first_res,
        jnp.ones((1, tokens.shape[1]), jnp.float32),
        1.0 + per_token[4],
        per_token[3],
        mlp_count,
        5,
    )
    hidden = product(
        mlp_in,
        up_full[None],
        0,
        1,
        256,
        jnp.bfloat16,
        functools.partial(jax.nn.gelu, approximate=True),
    )[0]
    hidden_all = line_gather(hidden, req_count, 6)
    units, columns = feedforward_down.shape
    down_part = jnp.dot(
        hidden_all.reshape(req_count * group_rows, units),
        feedforward_down,
        preferred_element_type=jnp.float32,
    ).astype(jnp.bfloat16)
    down_own = exit_rows(
        down_part.reshape(req_count, mlp_count, own_count, columns), mlp_count, req_count, 7
    )
    layer_out = (
        second_res.astype(jnp.float32) + per_token[5] * down_own.astype(jnp.float32)
    ).astype(jnp.bfloat16)
    return (layer_out, kv_pages)


def solution(mesh):
    return jax.shard_map(
        body,
        mesh=mesh,
        in_specs=(
            P(("req", "mlp"), None),
            P("req", None, None),
            P("req", None),
            P("req"),
            P(),
            P("mlp", None, None),
            P("mlp", None, None, None),
            P(None, None, "mlp"),
            P(None, "mlp"),
            P(None, "req"),
            P("req", None),
            P(None, "mlp", None),
            P(),
            P(None, "req", None, "mlp"),
            P("req", "mlp"),
            P("mlp", "req"),
        ),
        out_specs=(P(("req", "mlp"), None), P(None, "req", None, "mlp")),
        check_vma=False,
    )
```

```python
import functools
import math

import jax
import jax.numpy as jnp
from jax import lax
from jax.experimental import pallas as pl
from jax.experimental.pallas import tpu as pltpu
from jax.sharding import PartitionSpec as P

HD = 128
PAGE = 16


EPSILON = 1e-06


PAIR = 2
MESH = pl.DeviceIdType.MESH
ANY = pl.BlockSpec(memory_space=pl.ANY)
VM = pl.BlockSpec(memory_space=pltpu.VMEM)


def comm_call(kernel, out_shape, in_specs, out_specs, scratch, ident, room=4):
    return pl.pallas_call(
        kernel,
        out_shape=out_shape,
        in_specs=in_specs,
        out_specs=out_specs,
        scratch_shapes=scratch,
        compiler_params=pltpu.CompilerParams(
            collective_id=ident, has_side_effects=True, vmem_limit_bytes=room << 20
        ),
    )


def remote(source, target, send_sem, recv_sem, axis, place):
    return pltpu.make_async_remote_copy(
        src_ref=source,
        dst_ref=target,
        send_sem=send_sem,
        recv_sem=recv_sem,
        device_id={axis: place},
        device_id_type=MESH,
    )


def shift(me, step, count):
    return lax.rem(me + (step + count) % count, count)


def greet(peers):
    barrier = pltpu.get_barrier_semaphore()
    for axis, place in peers:
        pl.semaphore_signal(barrier, inc=1, device_id={axis: place}, device_id_type=MESH)
    pl.semaphore_wait(barrier, len(peers))


def pair_places(count):
    me = lax.axis_index("mlp")
    outer, core = lax.div(me, PAIR), lax.rem(me, PAIR)
    sibling = outer * PAIR + (PAIR - 1 - core)
    peers = [
        shift(outer, k, count // PAIR) * PAIR + core for k in range(count // PAIR)
    ]
    sources = [
        shift(outer, -k, count // PAIR) * PAIR + core for k in range(count // PAIR)
    ]
    return me, core, sibling, peers, sources


def gather_sems(count):
    steps = count // PAIR
    return [pltpu.SemaphoreType.DMA(())] + [pltpu.SemaphoreType.DMA((steps,))] * 4


def gather_rows(count, places, own_ref, out_ref, own_sem, send_sem, recv_sem, pass_send, pass_recv):
    me, core, sibling, peers, sources = places
    own = pltpu.make_async_copy(own_ref, out_ref.at[me], own_sem)
    sends = [
        remote(own_ref, out_ref.at[me], send_sem.at[k], recv_sem.at[k], "mlp", peers[k])
        for k in range(1, count // PAIR)
    ]
    for copy in sends:
        copy.start()
    passes = [remote(own_ref, out_ref.at[me], pass_send.at[0], pass_recv.at[0], "mlp", sibling)]
    passes[0].start()
    own.start()
    for k in range(1, count // PAIR):
        sends[k - 1].wait_recv()
        block = out_ref.at[sources[k]]
        passes.append(remote(block, block, pass_send.at[k], pass_recv.at[k], "mlp", sibling))
        passes[-1].start()
    for copy in sends:
        copy.wait_send()
    for copy in passes:
        copy.wait()
    own.wait()


def entry_kernel(count, tok_ref, scale_ref, shift_ref, maps_ref, out_ref, up_ref, norm, map_own, map_send, map_recv, *sems):
    places = pair_places(count)
    me = places[0]
    slots, width = maps_ref.shape[0], up_ref.shape[-1]
    others = [shift(me, k, count) for k in range(1, count)]
    greet([("mlp", place) for place in others])

    def columns(place):
        return maps_ref.at[:, :, :, pl.ds(pl.multiple_of(place * width, 128), width)]

    target = up_ref.at[pl.ds(me * slots, slots)]
    own = pltpu.make_async_copy(columns(me), target, map_own)
    own.start()
    copies = [
        remote(columns(place), target, map_send.at[k], map_recv.at[k], "mlp", place)
        for k, place in enumerate(others)
    ]
    norm[...] = (
        layer_norm(tok_ref[...].astype(jnp.float32)) * (1.0 + scale_ref[...]) + shift_ref[...]
    ).astype(jnp.bfloat16)
    for copy in copies:
        copy.start()
    gather_rows(count, places, norm, out_ref, *sems)
    for copy in copies:
        copy.wait()
    own.wait()


def entry_rows(tokens, scale, shift_rows, maps, count):
    rows, width = tokens.shape
    slots, two, rank, total = maps.shape
    dma = pltpu.SemaphoreType.DMA
    gathered, up = comm_call(
        functools.partial(entry_kernel, count),
        (
            jax.ShapeDtypeStruct((count, rows, width), jnp.bfloat16),
            jax.ShapeDtypeStruct((count * slots, two, rank, total // count), maps.dtype),
        ),
        [VM, VM, VM, ANY],
        (ANY, ANY),
        [pltpu.VMEM((rows, width), jnp.bfloat16), dma(()), dma((count - 1,)), dma((count - 1,))]
        + gather_sems(count),
        0,
        8,
    )(tokens, scale, shift_rows, maps)
    return gathered.reshape(count * rows, width), up


def sum_blocks(count, places, block_of, near, mid, far, ns, nr, fs, fr):
    me, core, sibling, peers, sources = places
    steps = count // PAIR
    order = list(range(1, steps)) + [0]
    pairs = {}
    for k in order:
        other = peers[k] + (PAIR - 1 - 2 * core)
        pairs[k] = remote(block_of(other), near.at[k], ns.at[k], nr.at[k], "mlp", sibling)
        pairs[k].start()
    sends = []
    for k in range(1, steps):
        pairs[k].wait_recv()
        mid[k] = (
            block_of(peers[k])[...].astype(jnp.float32) + near[k].astype(jnp.float32)
        ).astype(jnp.bfloat16)
        sends.append(remote(mid.at[k], far.at[k], fs.at[k], fr.at[k], "mlp", peers[k]))
        sends[-1].start()
    pairs[0].wait_recv()
    total = block_of(me)[...].astype(jnp.float32) + near[0].astype(jnp.float32)
    for k in range(1, steps):
        sends[k - 1].wait_recv()
        total = total + far[k].astype(jnp.float32)
    for k in order:
        pairs[k].wait_send()
    for copy in sends:
        copy.wait_send()
    return total


def sum_scratch(count, extent):
    steps = count // PAIR
    return [pltpu.VMEM((steps,) + extent, jnp.bfloat16)] * 3 + [
        pltpu.SemaphoreType.DMA((steps,))
    ] * 4


def middle_kernel(count, part_ref, base_ref, gate_ref, scale_ref, shift_ref, res_ref, out_ref, near, mid, far, norm, ns, nr, fs, fr, *sems):
    places = pair_places(count)
    greet([("mlp", places[2])] + [("mlp", place) for place in places[3][1:]])
    total = sum_blocks(
        count, places, lambda place: part_ref.at[place], near, mid, far, ns, nr, fs, fr
    )
    res = (base_ref[...].astype(jnp.float32) + gate_ref[...] * total).astype(jnp.bfloat16)
    res_ref[...] = res
    norm[...] = (layer_norm(res.astype(jnp.float32)) * scale_ref[...] + shift_ref[...]).astype(
        jnp.bfloat16
    )
    gather_rows(count, places, norm, out_ref, *sems)


def middle_rows(part, base, gate, scale, shift_rows, count, ident):
    rows, width = base.shape
    scratch = sum_scratch(count, (rows, width))
    res, gathered = comm_call(
        functools.partial(middle_kernel, count),
        (
            jax.ShapeDtypeStruct((rows, width), jnp.bfloat16),
            jax.ShapeDtypeStruct((count, rows, width), jnp.bfloat16),
        ),
        [VM] * 5,
        (VM, ANY),
        scratch[:3] + [pltpu.VMEM((rows, width), jnp.bfloat16)] + scratch[3:] + gather_sems(count),
        ident,
        24,
    )(part.reshape(count, rows, width), base, gate, scale, shift_rows)
    return res, gathered.reshape(count * rows, width)


def small_kernel(count, own_ref, out_ref, slots, send_sem, recv_sem):
    me = lax.axis_index("mlp")
    others = [shift(me, k, count) for k in range(1, count)]
    greet([("mlp", place) for place in others])
    copies = [
        remote(own_ref, slots.at[k], send_sem.at[k], recv_sem.at[k], "mlp", place)
        for k, place in enumerate(others)
    ]
    for copy in copies:
        copy.start()
    total = own_ref[...].astype(jnp.float32)
    for k, copy in enumerate(copies):
        copy.wait_recv()
        total = total + slots[k].astype(jnp.float32)
    out_ref[...] = total
    for copy in copies:
        copy.wait_send()


def small_sum(own, count, ident):
    dma = pltpu.SemaphoreType.DMA((count - 1,))
    return comm_call(
        functools.partial(small_kernel, count),
        jax.ShapeDtypeStruct(own.shape, jnp.float32),
        [VM],
        VM,
        [pltpu.VMEM((count - 1,) + own.shape, own.dtype), dma, dma],
        ident,
    )(own)


def line_kernel(count, own_ref, out_ref, own_sem, rs, rr, ls, lr):
    me = lax.axis_index("req")
    right, left = shift(me, 1, count), shift(me, -1, count)
    greet([("req", right), ("req", left)])
    own = pltpu.make_async_copy(own_ref, out_ref.at[me], own_sem)
    own.start()

    pieces = rs.shape[1]
    rows = own_ref.shape[0] // pieces

    def hop(step, piece, sign):
        block = jnp.clip(me - sign * step, 0, count - 1)
        part = pl.ds(piece * rows, rows)
        source = own_ref.at[part] if step == 0 else out_ref.at[block, part]
        send, recv, place = (rs, rr, right) if sign > 0 else (ls, lr, left)
        return remote(
            source,
            out_ref.at[block, part],
            send.at[step, piece],
            recv.at[step, piece],
            "req",
            place,
        )

    def each(step, work):
        for piece in range(pieces):
            work(step, piece)

    def advance(step, piece):
        if step > 0:

            @pl.when(me >= step)
            def _():
                hop(step - 1, piece, 1).wait_recv()

            @pl.when(me + step < count)
            def _():
                hop(step - 1, piece, -1).wait_recv()

        @pl.when((me >= step) & (me < count - 1))
        def _():
            hop(step, piece, 1).start()

        @pl.when((me + step < count) & (me > 0))
        def _():
            hop(step, piece, -1).start()

    def finish(step, piece):
        @pl.when(me >= count - 1)
        def _():
            hop(step, piece, 1).wait_recv()

        @pl.when(me < 1)
        def _():
            hop(step, piece, -1).wait_recv()

    def drain(step, piece):
        @pl.when((me >= step) & (me < count - 1))
        def _():
            hop(step, piece, 1).wait_send()

        @pl.when((me + step < count) & (me > 0))
        def _():
            hop(step, piece, -1).wait_send()

    for step in range(count - 1):
        each(step, advance)
    each(count - 2, finish)
    for step in range(count - 1):
        each(step, drain)
    own.wait()


def line_gather(own, count, ident):
    dma = pltpu.SemaphoreType.DMA
    return comm_call(
        functools.partial(line_kernel, count),
        jax.ShapeDtypeStruct((count,) + own.shape, own.dtype),
        [ANY],
        ANY,
        [dma(())] + [dma((count - 1, 4))] * 4,
        ident,
    )(own)


def exit_kernel(count, lines, part_ref, out_ref, near, mid, far, final, ns, nr, fs, fr, own_sem, send_sem, recv_sem):
    places = pair_places(count)
    me, core, sibling, peers, _ = places
    steps = count // PAIR
    line = lax.axis_index("req")
    groups = [shift(line, k + 1, lines) for k in range(lines)]
    greet(
        [("mlp", sibling)]
        + [("mlp", place) for place in peers[1:]]
        + [("req", place) for place in groups[:-1]]
    )
    order = list(range(1, steps)) + [0]
    pairs, sends, copies = {}, [], []
    for i, group in enumerate(groups):
        for k in order:
            other = peers[k] + (PAIR - 1 - 2 * core)
            pairs[i, k] = remote(
                part_ref.at[group, other], near.at[i, k], ns.at[i, k], nr.at[i, k], "mlp", sibling
            )
            pairs[i, k].start()
    for i, group in enumerate(groups):
        for k in range(1, steps):
            pairs[i, k].wait_recv()
            mid[i, k] = (
                part_ref[group, peers[k]].astype(jnp.float32) + near[i, k].astype(jnp.float32)
            ).astype(jnp.bfloat16)
            sends.append(
                remote(mid.at[i, k], far.at[i, k], fs.at[i, k], fr.at[i, k], "mlp", peers[k])
            )
            sends[-1].start()
    width = final.shape[-1]
    target = out_ref.at[:, pl.ds(pl.multiple_of(line * width, 128), width)]
    for i, group in enumerate(groups):
        pairs[i, 0].wait_recv()
        total = part_ref[group, me].astype(jnp.float32) + near[i, 0].astype(jnp.float32)
        for k in range(1, steps):
            sends[i * (steps - 1) + k - 1].wait_recv()
            total = total + far[i, k].astype(jnp.float32)
        final[i] = total.astype(jnp.bfloat16)
        if i < lines - 1:
            copies.append(
                remote(final.at[i], target, send_sem.at[i], recv_sem.at[i], "req", group)
            )
        else:
            copies.append(pltpu.make_async_copy(final.at[i], target, own_sem))
        copies[-1].start()
    for copy in list(pairs.values()) + sends:
        copy.wait_send()
    for copy in copies:
        copy.wait()


def exit_rows(part, count, lines, ident):
    groups, _, rows, width = part.shape
    steps = count // PAIR
    dma = pltpu.SemaphoreType.DMA
    return comm_call(
        functools.partial(exit_kernel, count, lines),
        jax.ShapeDtypeStruct((rows, lines * width), jnp.bfloat16),
        [VM],
        VM,
        [pltpu.VMEM((groups, steps, rows, width), jnp.bfloat16)] * 3
        + [pltpu.VMEM((groups, rows, width), jnp.bfloat16)]
        + [dma((groups, steps))] * 4
        + [dma(()), dma((lines - 1,)), dma((lines - 1,))],
        ident,
        24,
    )(part)


def layer_norm(values):
    center = values - jnp.mean(values, axis=-1, keepdims=True)
    spread = jnp.mean(center * center, axis=-1, keepdims=True)
    return center * lax.rsqrt(spread + EPSILON)


def rotary_tables(grid):
    half_dim = HD // 2
    spatial = half_dim // 3
    temporal = half_dim - 2 * spatial
    column = jnp.arange(HD, dtype=jnp.int32)
    sign = jnp.where(column < half_dim, -1.0, 1.0).astype(jnp.float32)
    column = column % half_dim
    which_axis = jnp.where(
        column < temporal, 0, jnp.where(column < temporal + spatial, 1, 2)
    ).astype(jnp.int32)
    offset = jnp.where(
        which_axis == 0, 0, jnp.where(which_axis == 1, temporal, temporal + spatial)
    ).astype(jnp.int32)
    span_size = jnp.where(which_axis == 0, temporal, spatial).astype(jnp.float32)
    frequency = jnp.exp(-(column - offset).astype(jnp.float32) / span_size * math.log(10000.0))
    grid = grid.astype(jnp.float32)[:, :, None]
    coordinate = jnp.where(
        which_axis == 0, grid[0], jnp.where(which_axis == 1, grid[1], grid[2])
    )
    angles = coordinate * frequency[None, :]
    return (jnp.cos(angles), jnp.sin(angles) * sign[None, :])


def attend(queries, key_rows, value_rows, allowed):
    scores = lax.dot_general(
        queries, key_rows, (((1,), (1,)), ((), ())), preferred_element_type=jnp.float32
    ) * (1.0 / math.sqrt(HD))
    weights = jnp.exp(jnp.where(allowed, scores, -1e30))
    weights = weights * (1.0 / jnp.sum(weights, axis=-1, keepdims=True))
    return jnp.dot(
        weights.astype(jnp.bfloat16), value_rows, preferred_element_type=jnp.float32
    ).astype(jnp.bfloat16)


def self_kernel(page_ref, q_ref, k_ref, v_ref, qs_ref, ks_ref, gain_ref, cos_ref, sin_ref, seg_ref, segs_ref, out_ref, kv_ref):
    cosine, sine = cos_ref[...], sin_ref[...]
    allowed = seg_ref[...] == segs_ref[...]

    def turned(ref, scale, gain, columns):
        rows = ref[:, columns] * scale * gain_ref[gain : gain + 1, columns]
        return (rows * cosine + pltpu.roll(rows, HD // 2, 1) * sine).astype(jnp.bfloat16)

    for head in range(q_ref.shape[1] // HD):
        columns = slice(head * HD, (head + 1) * HD)
        query = turned(q_ref, qs_ref[...], 0, columns)
        key = turned(k_ref, ks_ref[...], 1, columns)
        value = v_ref[:, columns]
        out_ref[:, columns] = attend(query, key, value, allowed)
        for block in range(kv_ref.shape[1]):
            page = page_ref[block]
            rows = slice(block * PAGE, (block + 1) * PAGE)
            kv_ref[0, page, :, columns] = key[rows]
            kv_ref[1, page, :, columns] = value[rows]


def self_attention(pages, query, key, value, query_scale, key_scale, gains, cosine, sine, segment):
    rows, width = query.shape
    return pl.pallas_call(
        self_kernel,
        out_shape=(
            jax.ShapeDtypeStruct((rows, width), jnp.bfloat16),
            jax.ShapeDtypeStruct((2, pages.shape[0], PAGE, width), jnp.bfloat16),
        ),
        in_specs=[pl.BlockSpec(memory_space=pltpu.SMEM)] + [VM] * 10,
        out_specs=(VM, VM),
        compiler_params=pltpu.CompilerParams(vmem_limit_bytes=16 << 20),
    )(
        pages,
        query,
        key,
        value,
        query_scale[:, None],
        key_scale[:, None],
        gains,
        cosine,
        sine,
        segment[:, None],
        segment[None, :],
    )


def cross_kernel(q_ref, k_ref, v_ref, seg_ref, owner_ref, out_ref):
    out_ref[...] = attend(q_ref[...], k_ref[0], v_ref[0], seg_ref[...] == owner_ref[...])


def cross_attention(query, cache, segment, owner):
    rows, width = query.shape
    texts = cache.shape[1]
    head = pl.BlockSpec((rows, HD), lambda h: (0, h))
    return pl.pallas_call(
        cross_kernel,
        out_shape=jax.ShapeDtypeStruct((rows, width), jnp.bfloat16),
        grid=(width // HD,),
        in_specs=[
            head,
            pl.BlockSpec((1, texts, HD), lambda h: (0, 0, h)),
            pl.BlockSpec((1, texts, HD), lambda h: (1, 0, h)),
            pl.BlockSpec((rows, 1), lambda h: (0, 0)),
            pl.BlockSpec((1, texts), lambda h: (0, 0)),
        ],
        out_specs=head,
        compiler_params=pltpu.CompilerParams(vmem_limit_bytes=24 << 20),
    )(query, cache, cache, segment[:, None], owner[None, :])


def product_kernel(act, x_ref, w_ref, out_ref):
    out_ref[0] = act(
        jnp.dot(x_ref[...], w_ref[0], preferred_element_type=jnp.float32)
    ).astype(out_ref.dtype)


def product(rows_in, maps, first, amount, tile, dtype, act=lambda part: part):
    rows, depth = rows_in.shape
    width = maps.shape[2]
    tile = min(tile, width)
    return pl.pallas_call(
        functools.partial(product_kernel, act),
        out_shape=jax.ShapeDtypeStruct((amount, rows, width), dtype),
        grid=(amount, width // tile),
        in_specs=[
            pl.BlockSpec((rows, depth), lambda i, j: (0, 0)),
            pl.BlockSpec((1, depth, tile), lambda i, j: (first + i, 0, j)),
        ],
        out_specs=pl.BlockSpec((1, rows, tile), lambda i, j: (i, 0, j)),
        compiler_params=pltpu.CompilerParams(vmem_limit_bytes=24 << 20),
    )(rows_in, pltpu.with_memory_space_constraint(maps, pltpu.HBM))


def choose_rows(table, segment):
    chosen = jnp.zeros((segment.shape[0],) + table.shape[1:], table.dtype)
    for request in range(table.shape[0]):
        picked = (segment == request).reshape((-1,) + (1,) * (table.ndim - 1))
        chosen = jnp.where(picked, table[request][None], chosen)
    return chosen


def body(
    tokens,
    modulation,
    lengths,
    request_adapter,
    adapter_storage,
    adapter_down_weight,
    adapter_up_maps,
    input_projection,
    query_key_gains,
    positions,
    block_page_lookup,
    output_projection,
    cross_norm_gain,
    text_token_cache,
    feedforward_up,
    feedforward_down,
):
    mlp_count = lax.axis_size("mlp")
    my_index = lax.axis_index("mlp")
    own_count = tokens.shape[0]
    group_rows = own_count * mlp_count
    local_width = input_projection.shape[2]
    entire_width = local_width * mlp_count
    resident_slots = adapter_down_weight.shape[0]
    doubled_rank = adapter_down_weight.shape[2]
    rank_once = doubled_rank // 2

    req_count = lax.axis_size("req")
    slot_total = resident_slots * mlp_count
    up_full = lax.all_gather(feedforward_up, "req", axis=0, tiled=True)
    bounds = jnp.cumsum(lengths[0])
    position = jnp.arange(group_rows, dtype=jnp.int32)
    segment = jnp.sum((position[:, None] >= bounds[None, :]).astype(jnp.int32), axis=1)
    own_start = my_index * own_count
    own_segment = lax.dynamic_slice_in_dim(segment, own_start, own_count)
    per_token = [choose_rows(modulation[:, which_row, :], own_segment) for which_row in range(6)]
    token_f32 = tokens.astype(jnp.float32)
    rows_in, adapter_up_weight = entry_rows(
        tokens, per_token[1], per_token[0], adapter_up_maps, mlp_count
    )
    request_slot = adapter_storage[request_adapter]
    token_slot = jnp.sum(
        jnp.where(
            segment[:, None] == jnp.arange(request_slot.shape[0], dtype=jnp.int32)[None, :],
            request_slot[None, :],
            0,
        ),
        axis=1,
    )
    resident = my_index * resident_slots + jnp.arange(resident_slots, dtype=jnp.int32)
    held = (token_slot[None, :] == resident[:, None]).astype(jnp.float32)
    code_block = lax.dot_general(
        adapter_down_weight.transpose(0, 2, 1).reshape(resident_slots * doubled_rank, -1),
        rows_in,
        (((1,), (1,)), ((), ())),
        preferred_element_type=jnp.float32,
    ).reshape(resident_slots, doubled_rank, group_rows)
    my_codes = jnp.sum(held[:, None, :] * code_block, axis=0).astype(jnp.bfloat16)
    codes = small_sum(my_codes, mlp_count, 1).astype(jnp.bfloat16)
    slots = jnp.arange(slot_total, dtype=jnp.int32)
    everywhere = token_slot[None, :] == slots[:, None]

    def spread(code_part):
        return jnp.where(everywhere[:, None, :], code_part[None], jnp.bfloat16(0)).reshape(
            slot_total * rank_once, group_rows
        )

    def adapted(code_part, which_map):
        return lax.dot_general(
            spread(code_part),
            adapter_up_weight[:, which_map].reshape(slot_total * rank_once, local_width),
            (((0,), (0,)), ((), ())),
            preferred_element_type=jnp.float32,
        )

    projected = product(rows_in, input_projection, 0, 3, 256, jnp.float32)
    query_linear = projected[0] + adapted(codes[:rank_once], 0)
    key_linear = projected[1]
    value_rows = (projected[2] + adapted(codes[rank_once:], 1)).astype(jnp.bfloat16)
    squares = small_sum(
        jnp.stack(
            [jnp.sum(query_linear * query_linear, axis=1), jnp.sum(key_linear * key_linear, axis=1)]
        ),
        mlp_count,
        2,
    )
    query_square, key_square = squares[0], squares[1]
    cosine, sine = rotary_tables(positions)
    attended, kv_pages = self_attention(
        block_page_lookup[0],
        query_linear,
        key_linear,
        value_rows,
        lax.rsqrt(query_square / entire_width + EPSILON),
        lax.rsqrt(key_square / entire_width + EPSILON),
        query_key_gains,
        cosine,
        sine,
        segment,
    )
    text_owner = (
        jnp.arange(text_token_cache.shape[1] * text_token_cache.shape[2], dtype=jnp.int32)
        // text_token_cache.shape[2]
    )

    def out_rows(rows, which_map):
        return product(rows, output_projection, which_map, 1, 1280, jnp.bfloat16)[0]

    first_res, cross_in = middle_rows(
        out_rows(attended, 0),
        tokens,
        per_token[2],
        cross_norm_gain[None, :],
        jnp.zeros((1, tokens.shape[1]), jnp.float32),
        mlp_count,
        3,
    )
    cross_linear = product(cross_in, input_projection, 3, 1, 256, jnp.float32)[0]
    cross_square = small_sum(
        jnp.sum(cross_linear * cross_linear, axis=1)[None, :], mlp_count, 4
    )[0]
    cross_query = (
        cross_linear
        * lax.rsqrt(cross_square / entire_width + EPSILON)[:, None]
        * query_key_gains[2]
    ).astype(jnp.bfloat16)
    cross_out = cross_attention(
        cross_query,
        text_token_cache.reshape(2, text_owner.shape[0], local_width),
        segment,
        text_owner,
    )
    second_res, mlp_in = middle_rows(
        out_rows(cross_out, 1),
        first_res,
        jnp.ones((1, tokens.shape[1]), jnp.float32),
        1.0 + per_token[4],
        per_token[3],
        mlp_count,
        5,
    )
    hidden = product(
        mlp_in,
        up_full[None],
        0,
        1,
        256,
        jnp.bfloat16,
        functools.partial(jax.nn.gelu, approximate=True),
    )[0]
    hidden_all = line_gather(hidden, req_count, 6)
    units, columns = feedforward_down.shape
    down_part = jnp.dot(
        hidden_all.reshape(req_count * group_rows, units),
        feedforward_down,
        preferred_element_type=jnp.float32,
    ).astype(jnp.bfloat16)
    down_own = exit_rows(
        down_part.reshape(req_count, mlp_count, own_count, columns), mlp_count, req_count, 7
    )
    layer_out = (
        second_res.astype(jnp.float32) + per_token[5] * down_own.astype(jnp.float32)
    ).astype(jnp.bfloat16)
    return (layer_out, kv_pages)


def solution(mesh):
    return jax.shard_map(
        body,
        mesh=mesh,
        in_specs=(
            P(("req", "mlp"), None),
            P("req", None, None),
            P("req", None),
            P("req"),
            P(),
            P("mlp", None, None),
            P("mlp", None, None, None),
            P(None, None, "mlp"),
            P(None, "mlp"),
            P(None, "req"),
            P("req", None),
            P(None, "mlp", None),
            P(),
            P(None, "req", None, "mlp"),
            P("req", "mlp"),
            P("mlp", "req"),
        ),
        out_specs=(P(("req", "mlp"), None), P(None, "req", None, "mlp")),
        check_vma=False,
    )
```
